256 devices in a mesh: band: 32 (over y, x, core), slab: 8 (over z).
Axes of the slice: x: 4, y: 4, z: 8, core: 2. Of those that a mesh axis runs over, the one named last changes fastest.
Arguments:
- orbitals: float32 [32, 128, 128, 128], P('band', 'slab'), may hold values from -6 to 6
- column_ids: int32 [8, 768], P('slab'), may hold values from 0 to 4095, as said below
- source_ids: int32 [2], replicated, may hold values from 0 to 31
Outputs:
- exchange: float32 [32, 128, 128, 128], P('band', 'slab')
- energy: float32 [32, 6144], P('band', 'slab')
The draws below stay inside these ranges and needn't reach their ends.
Inputs may be any that keep to these rules, and one draw needn't show every extreme that they name: `column_ids`: A column is numbered c = (ky + 32) * 64 + kz + 32. Every column with ky^2 + kz^2 < 32^2 appears exactly once in the whole table; every other slot holds 0, a column outside that disk. One row holds 768 such disk columns.
All inputs are finite; a program needn't handle non-finite values.
Results may differ from the reference program's by a relative error of at most 0.0001.
Values sent between devices are 32-bit elements; how exact they have to be, the bound alone decides.
No kernel may reach another device: no remote copies, remote signals or barrier semaphores. Data moves between devices by JAX's collectives and lax.ppermute only.
A program may use at most 128 MiB of HBM per device.

```python
import jax
import jax.numpy as jnp
import numpy as np
from jax import lax

G = 128
KCUT = 32
KB = 64
CMAX = 768
ORBITALS = 32
SOURCES = 2
N_SLAB = 8


def draw_column_ids(key, part):
    wave = np.arange(KB) - KCUT
    inside = (wave[:, None] ** 2 + wave[None, :] ** 2 < KCUT * KCUT).reshape(-1)
    disk_count = int(np.sum(inside))
    outside_score = jnp.asarray(1 - inside.astype(np.int32), dtype=jnp.int32)
    disk_ids = jnp.argsort(outside_score, stable=True)[:disk_count].astype(jnp.int32)
    key_order, key_heavy = jax.random.split(jax.random.fold_in(key, 11))
    shuffled = jax.random.permutation(key_order, disk_ids)
    heavy = jax.random.randint(key_heavy, (), 0, N_SLAB, dtype=jnp.int32)
    ranks = jnp.arange(disk_count, dtype=jnp.int32)
    others = (heavy + 1 + (ranks - CMAX) % (N_SLAB - 1)) % N_SLAB
    owner = jnp.where(ranks < CMAX, heavy, others)
    slot = jnp.where(ranks < CMAX, ranks, (ranks - CMAX) // (N_SLAB - 1))
    table = jnp.zeros((N_SLAB, CMAX), jnp.int32)
    return table.at[owner, slot].set(shuffled)


def shard_levels(key, shape, cuts, least, high):
    def one(dim, blocks):
        steps = jax.random.uniform(jax.random.fold_in(jax.random.fold_in(key, 6), dim), (blocks,), jnp.float32, least / len(cuts), high / len(cuts))
        return jnp.repeat(jnp.exp(steps), shape[dim] // blocks).reshape((-1,) + (1,) * (len(shape) - dim - 1))

    loudness = one(*cuts[0])
    for cut in cuts[1:]:
        loudness = loudness * one(*cut)
    return loudness


def bell_draw(key, dims, spread, reach, shards=(), kind=jnp.bfloat16):
    values = jax.random.normal(key, dims, jnp.float32) * spread
    if len(shards) > 0:
        values = shard_levels(key, dims, shards, -0.22, 0.18) * values
    return jnp.clip(values, min=-reach, max=reach).astype(kind)


def setup_inputs(seed: int = 0) -> dict:
    seeds = jax.random.split(jax.random.key(seed), 4)
    return {
        "orbitals": bell_draw(seeds[0], (ORBITALS, G, G, G), 1.0, 6.0, ((0, 32), (1, 8)), jnp.float32),
        "column_ids": draw_column_ids(jax.random.fold_in(seeds[3], 71), 0),
        "source_ids": jax.random.randint(seeds[2], (SOURCES,), 0, ORBITALS).astype(jnp.int32),
    }


def reference(orbitals, column_ids, source_ids):
    wave = (jnp.arange(G, dtype=jnp.int32) + G // 2) % G - G // 2
    half_wave = jnp.arange(G // 2 + 1, dtype=jnp.int32)
    radius = wave[:, None, None] ** 2 + wave[None, :, None] ** 2 + half_wave[None, None, :] ** 2
    kernel_table = jnp.where(radius < KCUT * KCUT, 4.0 / (1.0 + radius.astype(jnp.float32) / 1024.0), 0.0).astype(jnp.float32)
    scale = float(G) ** 1.5
    sources = orbitals[source_ids]

    def per_orbital(orbital):
        def per_source(carry, source):
            exchange, col_power = carry
            spectrum = jnp.fft.rfftn(source * orbital) / scale
            potential = jnp.fft.irfftn(spectrum * kernel_table, s=(G, G, G)) * scale
            magnitude = spectrum.real * spectrum.real + spectrum.imag * spectrum.imag
            col_power = col_power + jnp.sum(kernel_table * magnitude, axis=0) / KB
            return (exchange + source * potential, col_power), None

        start = (jnp.zeros((G, G, G), jnp.float32), jnp.zeros((G, G // 2 + 1), jnp.float32))
        result, _ = lax.scan(per_source, start, sources)
        return result

    exchange, col_power = lax.map(per_orbital, orbitals)
    slot_ids = column_ids.reshape(-1).astype(jnp.int32)
    wave_y = slot_ids // KB - KCUT
    wave_z = slot_ids % KB - KCUT
    flipped = wave_z < 0
    row_index = jnp.where(flipped, (-wave_y) % G, wave_y % G).astype(jnp.int32)
    col_index = jnp.where(flipped, -wave_z, wave_z).astype(jnp.int32)
    energy = col_power[:, row_index, col_index]
    return exchange, energy
```

```python
import functools
import math

import jax
import jax.numpy as jnp
import numpy as np
from jax import lax
from jax.experimental import pallas as pl
from jax.experimental.pallas import tpu as pltpu
from jax.sharding import PartitionSpec as P

G = 128
KCUT = 32
SLABS = 8
PLANES = 16
SLOTS = 768
ROWS = 8
LANES = 128


def split_table(table):
    high = table.astype(jnp.bfloat16)
    low = (table - high.astype(np.float64)).astype(jnp.bfloat16)
    return high, low


def waves(points):
    phase = np.arange(KCUT)[:, None] * np.arange(points)[None, :] % points
    angle = phase * (2.0 * math.pi / points)
    return np.cos(angle), np.sin(angle)


def basis_tables():
    cosine, sine = waves(G)
    along_x = np.concatenate([cosine, sine], axis=0)
    group_rows = []
    for slab in range(SLABS):
        group_rows.append(cosine[4 * slab : 4 * slab + 4])
        group_rows.append(sine[4 * slab : 4 * slab + 4])
    along_y = np.concatenate(group_rows, axis=0)
    along_z = np.zeros((2 * G, LANES))
    along_z[:G, :64] = along_x.T
    along_z[G:, 64:] = along_x.T
    return along_x, along_y, along_z


def bf16_parts(value):
    high = value.astype(jnp.bfloat16)
    low = (value - high.astype(jnp.float32)).astype(jnp.bfloat16)
    return high, low


def dot(a, b):
    return jnp.dot(a, b, preferred_element_type=jnp.float32)


def left_product(stacked, value):
    high, low = bf16_parts(value)
    rows = stacked.shape[0] // 2
    first = dot(stacked, high)
    return first[:rows] + first[rows:] + dot(stacked[:rows], low)


def forward_kernel(place_ref, orbital_ref, ty_ref, tz_ref, *refs):
    piece_refs, out_ref = refs[:-1], refs[-1]
    for p, piece_ref in enumerate(piece_refs):
        plane = place_ref[p] * 2
        orbital = orbital_ref[0, pl.ds(plane, 2)]
        pair0 = (piece_ref[0] * orbital).reshape(2 * G, G)
        pair1 = (piece_ref[1] * orbital).reshape(2 * G, G)
        high, low = bf16_parts(jnp.concatenate([pair0, pair1], axis=1))
        first = dot(high, tz_ref[...])
        along_z = first[:, :LANES] + first[:, LANES:] + dot(low, tz_ref[:, :LANES])
        for q in range(2):
            box = left_product(ty_ref[...], along_z[q * G : (q + 1) * G])
            out_ref[:, plane + q] = box.reshape(SLABS, ROWS, LANES)


def filter_kernel(slab_ref, cols_ref, tx_ref, txt_ref, out_ref):
    lane = lax.broadcasted_iota(jnp.int32, (2 * KCUT, LANES), 1)
    row = lax.broadcasted_iota(jnp.int32, (2 * KCUT, LANES), 0)
    wave_z = lane % KCUT
    wave_x = row % KCUT
    scale = float(G) ** -3
    many_x = jnp.where(wave_x == 0, 1.0, 2.0)
    many_z = jnp.where(wave_z == 0, 1.0, 2.0)
    power_rows = []
    for j in range(4):
        wave_y = slab_ref[0] * 4 + j
        radius = wave_x * wave_x + wave_z * wave_z + wave_y * wave_y
        weight = jnp.where(
            radius < KCUT * KCUT, (4.0 * scale) / (1.0 + radius.astype(jnp.float32) / 1024.0), 0.0
        )
        weight = weight * many_x
        many_y = jnp.where(wave_y == 0, 1.0, 2.0)
        spread = weight * (many_z * many_y)
        cos_y = left_product(tx_ref[...], cols_ref[:, j, :])
        sin_y = left_product(tx_ref[...], cols_ref[:, j + 4, :])
        squares = jnp.sum(weight * (cos_y * cos_y + sin_y * sin_y), axis=0, keepdims=True)
        cross = cos_y * pltpu.roll(sin_y, 96, 1) - sin_y * pltpu.roll(cos_y, 96, 1)
        cross = 2.0 * jnp.sum(weight * cross, axis=0, keepdims=True)
        squares = squares + pltpu.roll(squares, 96, 1)
        same = squares - cross
        other = squares + cross
        same = same + pltpu.roll(same, 64, 1)
        other = other + pltpu.roll(other, 64, 1)
        first = lax.broadcasted_iota(jnp.int32, (1, LANES), 1) < KCUT
        power_rows.append(jnp.where(first, same, pltpu.roll(other, 32, 1)) * (1.0 / 64.0))
        for k, value in ((j, cos_y), (j + 4, sin_y)):
            back = left_product(txt_ref[...], spread * value)
            for d in range(SLABS):
                out_ref[d, 0:PLANES, k, :] = back[d * PLANES : (d + 1) * PLANES]
    power = jnp.concatenate(power_rows + power_rows, axis=0)
    for d in range(SLABS):
        out_ref[d, PLANES] = power


def inverse_kernel(place_ref, back_ref, ids_ref, ty_ref, tz_ref, *refs):
    piece_refs, exchange_ref, energy_ref = refs[:-2], refs[-2], refs[-1]
    for p, piece_ref in enumerate(piece_refs):
        plane = place_ref[p] * 2
        rows = []
        for q in range(2):
            box = back_ref[:, plane + q].reshape(SLABS * ROWS, LANES)
            rows.append(left_product(ty_ref[...], box))
        high, low = bf16_parts(jnp.concatenate(rows, axis=0))
        pots = dot(high, tz_ref[0]) + dot(low, tz_ref[0]) + dot(high, tz_ref[1])
        value = piece_ref[0].reshape(2 * G, G) * pots[:, :G] + piece_ref[1].reshape(2 * G, G) * pots[:, G:]
        exchange_ref[0, pl.ds(plane, 2)] = value.reshape(2, G, G)
    power = back_ref[:, PLANES].reshape(SLABS * ROWS, LANES)
    ids = ids_ref[...]
    wave_y = ids // 64 - KCUT
    wave_z = ids % 64 - KCUT
    size_y = jnp.abs(wave_y)
    size_z = jnp.abs(wave_z)
    row = jnp.where(size_y < KCUT, (size_y // 4) * ROWS + size_y % 4, -1)
    pick = jnp.where(wave_y * wave_z < 0, size_z + KCUT, size_z)
    pick = jnp.where(size_z < KCUT, pick, -1)
    hot = (lax.broadcasted_iota(jnp.int32, (SLABS * ROWS, SLOTS), 0) == row).astype(jnp.bfloat16)
    transposed = power.T
    high, low = bf16_parts(transposed)
    rest = (transposed - high.astype(jnp.float32) - low.astype(jnp.float32)).astype(jnp.bfloat16)
    table = dot(high, hot) + dot(low, hot) + dot(rest, hot)
    lane = lax.broadcasted_iota(jnp.int32, (LANES, SLOTS), 0)
    energy_ref[...] = jnp.sum(jnp.where(lane == pick, table, 0.0), axis=0, keepdims=True)


VMEM = pl.BlockSpec(memory_space=pltpu.VMEM)
SMEM = pl.BlockSpec(memory_space=pltpu.SMEM)


def band_index(y, x, core):
    return (y * 4 + x) * 2 + core


def gray(place):
    return place ^ (place >> 1)


PLACE_OF_CODE = [0, 1, 3, 2]


def neighbour(y, x, dim):
    code = gray(x) | (gray(y) << 2)
    code = code ^ (1 << dim)
    return PLACE_OF_CODE[code >> 2], PLACE_OF_CODE[code & 3]


def cube_pairs(slot, step):
    pairs = []
    for y in range(4):
        for x in range(4):
            for core in range(2):
                there = neighbour(y, x, (2 * core + slot + step) % 4)
                pairs.append((band_index(y, x, core), band_index(*there, core)))
    return pairs


CORE_PAIRS = [(i, i ^ 1) for i in range(32)]


def bit(code, position):
    return (code >> position) & 1


def broadcast_sources(orbitals, source_ids):
    me = lax.axis_index("band")
    core = me % 2
    x = (me // 2) % 4
    y = me // 8
    code = gray(x) | (gray(y) << 2)
    orbital = orbitals[0].reshape(2, 2, 2, 2, G, G)
    mine = lax.dynamic_index_in_dim(orbital, core, 0, keepdims=False)
    theirs = lax.ppermute(
        lax.dynamic_index_in_dim(orbital, 1 - core, 0, keepdims=False), "band", CORE_PAIRS
    )
    source_x = (source_ids // 2) % 4
    source_y = source_ids // 8
    relative = code ^ (gray(source_x) | (gray(source_y) << 2))
    is_mine = (source_ids % 2 == core)[:, None, None, None]

    def choose(flags, one, two):
        return jnp.where(flags[:, None, None, None], one, two)

    keeps, gots, places, partner_places = [], [], [], []
    for slot in range(2):
        side = bit(code, (2 * core + slot) % 4)

        def half(which, slot=slot):
            own = lax.dynamic_index_in_dim(mine[slot], which, 0, keepdims=False)
            other = lax.dynamic_index_in_dim(theirs[slot], which, 0, keepdims=False)
            return jnp.where(is_mine, own[None], other[None])

        got = lax.ppermute(half(1 - side), "band", cube_pairs(slot, 0))
        keep = choose(relative == 0, half(side), got)
        keeps.append(keep)
        partner_side = bit(code, (2 * (1 - core) + slot) % 4)
        places.append((4 * core + 2 * slot + side, 4 * core + 2 * slot + 1 - side))
        base = 4 * (1 - core) + 2 * slot
        partner_places.append((base + partner_side, base + 1 - partner_side))
    for step in range(1, 4):
        for slot in range(2):
            got = lax.ppermute(keeps[slot], "band", cube_pairs(slot, step))
            flags = bit(relative, (2 * core + slot + step) % 4) == 1
            keeps[slot] = choose(flags, got, keeps[slot])
    gots = [lax.ppermute(keeps[slot], "band", cube_pairs(slot, 0)) for slot in range(2)]
    swapped = [lax.ppermute(keeps[slot], "band", CORE_PAIRS) for slot in range(2)]
    swapped_gots = [lax.ppermute(gots[slot], "band", CORE_PAIRS) for slot in range(2)]
    pieces = keeps + swapped + gots + swapped_gots
    order = [p[0] for p in places] + [p[0] for p in partner_places]
    order += [p[1] for p in places] + [p[1] for p in partner_places]
    return pieces, jnp.stack(order).astype(jnp.int32)


def call(kernel, specs, shapes, name):
    single = isinstance(shapes, jax.ShapeDtypeStruct)
    return pl.pallas_call(
        kernel,
        out_shape=shapes,
        in_specs=specs,
        out_specs=VMEM if single else tuple(VMEM for _ in shapes),
        name=name,
        compiler_params=pltpu.CompilerParams(vmem_limit_bytes=32 << 20),
    )


def body(orbitals, column_ids, source_ids):
    along_x, along_y, along_z = basis_tables()
    forward_y = jnp.asarray(np.concatenate(split_table(along_y), axis=0))
    forward_z = jnp.asarray(np.concatenate(split_table(along_z), axis=1))
    forward_x = jnp.asarray(np.concatenate(split_table(along_x), axis=0))
    inverse_x = jnp.asarray(np.concatenate(split_table(along_x.T), axis=0))
    inverse_y = jnp.asarray(np.concatenate(split_table(along_y.T), axis=0))
    inverse_z = jnp.asarray(np.stack(split_table(along_z.T), axis=0))

    pieces, places = broadcast_sources(orbitals, source_ids)
    f32 = jnp.float32
    columns = call(
        forward_kernel,
        [SMEM] + [VMEM] * (3 + len(pieces)),
        jax.ShapeDtypeStruct((SLABS, PLANES, ROWS, LANES), f32),
        "forward",
    )(places, orbitals, forward_y, forward_z, *pieces)
    columns = lax.all_to_all(columns, "slab", 0, 0, tiled=True)
    slab = lax.axis_index("slab").astype(jnp.int32).reshape(1)
    back = call(
        filter_kernel,
        [SMEM] + [VMEM] * 3,
        jax.ShapeDtypeStruct((SLABS, PLANES + 1, ROWS, LANES), f32),
        "filter",
    )(slab, columns.reshape(SLABS * PLANES, ROWS, LANES), forward_x, inverse_x)
    back = lax.all_to_all(back, "slab", 0, 0, tiled=True)
    exchange, energy = call(
        inverse_kernel,
        [SMEM] + [VMEM] * (4 + len(pieces)),
        (
            jax.ShapeDtypeStruct((1, PLANES, G, G), f32),
            jax.ShapeDtypeStruct((1, SLOTS), f32),
        ),
        "inverse",
    )(places, back, column_ids, inverse_y, inverse_z, *pieces)
    return exchange, energy


def solution(mesh):
    placed = (P("band", "slab", None, None), P("slab", None), P())
    return jax.shard_map(
        body,
        mesh=mesh,
        in_specs=placed,
        out_specs=(P("band", "slab", None, None), P("band", "slab")),
        check_vma=False,
    )
```

```python
import math

import jax
import jax.numpy as jnp
import numpy as np
from jax import lax
from jax.experimental import pallas as pl
from jax.experimental.pallas import tpu as pltpu
from jax.sharding import PartitionSpec as P

G = 128
KCUT = 32
SLABS = 8
PLANES = 16
SLOTS = 768
ROWS = 8
LANES = 128


def split_table(table):
    high = table.astype(jnp.bfloat16)
    low = (table - high.astype(np.float64)).astype(jnp.bfloat16)
    return high, low


def waves(points):
    phase = np.arange(KCUT)[:, None] * np.arange(points)[None, :] % points
    angle = phase * (2.0 * math.pi / points)
    return np.cos(angle), np.sin(angle)


def basis_tables():
    cosine, sine = waves(G)
    along_x = np.concatenate([cosine, sine], axis=0)
    group_rows = []
    for slab in range(SLABS):
        group_rows.append(cosine[4 * slab : 4 * slab + 4])
        group_rows.append(sine[4 * slab : 4 * slab + 4])
    along_y = np.concatenate(group_rows, axis=0)
    along_z = np.zeros((2 * G, LANES))
    along_z[:G, :64] = along_x.T
    along_z[G:, 64:] = along_x.T
    return along_x, along_y, along_z


def bf16_parts(value):
    high = value.astype(jnp.bfloat16)
    low = (value - high.astype(jnp.float32)).astype(jnp.bfloat16)
    return high, low


def dot(a, b):
    return jnp.dot(a, b, preferred_element_type=jnp.float32)


def left_product(stacked, value):
    high, low = bf16_parts(value)
    rows = stacked.shape[0] // 2
    first = dot(stacked, high)
    return first[:rows] + first[rows:] + dot(stacked[:rows], low)


def wide_product(joined, value):
    high, low = bf16_parts(value)
    table = jnp.concatenate([joined, joined[:, :64]], axis=1)
    return dot(table, jnp.concatenate([high, high, low], axis=0))


def forward_kernel(place_ref, orbital_ref, ty_ref, tz_ref, *refs):
    piece_refs, out_refs = refs[:-SLABS], refs[-SLABS:]
    for p, piece_ref in enumerate(piece_refs):
        plane = place_ref[p] * 2
        orbital = orbital_ref[0, pl.ds(plane, 2)]
        pair0 = (piece_ref[0] * orbital).reshape(2 * G, G)
        pair1 = (piece_ref[1] * orbital).reshape(2 * G, G)
        high, low = bf16_parts(jnp.concatenate([pair0, pair1], axis=1))
        first = dot(high, tz_ref[...])
        along_z = first[:, :LANES] + first[:, LANES:] + dot(low, tz_ref[:, :LANES])
        for q in range(2):
            box = left_product(ty_ref[...], along_z[q * G : (q + 1) * G])
            for k in range(SLABS):
                out_refs[k][plane + q] = box[k * ROWS : (k + 1) * ROWS]


def filter_kernel(slab_ref, tx_ref, txt_ref, *refs):
    cols_refs, out_refs = refs[:SLABS], refs[SLABS:]

    def columns(j):
        return jnp.concatenate([ref[:, j, :] for ref in cols_refs], axis=0)

    lane = lax.broadcasted_iota(jnp.int32, (2 * KCUT, LANES), 1)
    row = lax.broadcasted_iota(jnp.int32, (2 * KCUT, LANES), 0)
    wave_z = lane % KCUT
    wave_x = row % KCUT
    scale = float(G) ** -3
    many_x = jnp.where(wave_x == 0, 1.0, 2.0)
    many_z = jnp.where(wave_z == 0, 1.0, 2.0)
    power_rows = []
    for j in range(4):
        wave_y = slab_ref[0] * 4 + j
        radius = wave_x * wave_x + wave_z * wave_z + wave_y * wave_y
        weight = jnp.where(
            radius < KCUT * KCUT, (4.0 * scale) / (1.0 + radius.astype(jnp.float32) / 1024.0), 0.0
        )
        weight = weight * many_x
        many_y = jnp.where(wave_y == 0, 1.0, 2.0)
        spread = weight * (many_z * many_y)
        cos_y = left_product(tx_ref[...], columns(j))
        sin_y = left_product(tx_ref[...], columns(j + 4))
        squares = jnp.sum(weight * (cos_y * cos_y + sin_y * sin_y), axis=0, keepdims=True)
        cross = cos_y * pltpu.roll(sin_y, 96, 1) - sin_y * pltpu.roll(cos_y, 96, 1)
        cross = 2.0 * jnp.sum(weight * cross, axis=0, keepdims=True)
        squares = squares + pltpu.roll(squares, 96, 1)
        same = squares - cross
        other = squares + cross
        same = same + pltpu.roll(same, 64, 1)
        other = other + pltpu.roll(other, 64, 1)
        first = lax.broadcasted_iota(jnp.int32, (1, LANES), 1) < KCUT
        power_rows.append(jnp.where(first, same, pltpu.roll(other, 32, 1)) * (1.0 / 64.0))
        for k, value in ((j, cos_y), (j + 4, sin_y)):
            back = wide_product(txt_ref[...], spread * value)
            for d in range(SLABS):
                out_refs[d][0:PLANES, k, :] = back[d * PLANES : (d + 1) * PLANES]
    power = jnp.concatenate(power_rows + power_rows, axis=0)
    for d in range(SLABS):
        out_refs[d][PLANES] = power


def inverse_kernel(place_ref, slab_ref, ids_ref, ty_ref, tz_ref, *refs):
    back_refs, piece_refs, exchange_ref, energy_ref = refs[:SLABS], refs[SLABS:-2], refs[-2], refs[-1]
    for p, piece_ref in enumerate(piece_refs):
        plane = place_ref[p] * 2
        rows = []
        for q in range(2):
            box = jnp.concatenate([ref[plane + q] for ref in back_refs], axis=0)
            rows.append(wide_product(ty_ref[...], box))
        high, low = bf16_parts(jnp.concatenate(rows, axis=0))
        pots = dot(high, tz_ref[0]) + dot(low, tz_ref[0]) + dot(high, tz_ref[1])
        value = piece_ref[0].reshape(2 * G, G) * pots[:, :G] + piece_ref[1].reshape(2 * G, G) * pots[:, G:]
        exchange_ref[0, pl.ds(plane, 2)] = value.reshape(2, G, G)
    power = jnp.concatenate([ref[PLANES] for ref in back_refs], axis=0)
    ids = ids_ref[...]
    wave_y = ids // 64 - KCUT
    wave_z = ids % 64 - KCUT
    size_y = jnp.abs(wave_y)
    size_z = jnp.abs(wave_z)
    group = (size_y // 4 + SLABS - slab_ref[0]) % SLABS
    row = jnp.where(size_y < KCUT, group * ROWS + size_y % 4, -1)
    pick = jnp.where(wave_y * wave_z < 0, size_z + KCUT, size_z)
    pick = jnp.where(size_z < KCUT, pick, -1)
    hot = (lax.broadcasted_iota(jnp.int32, (SLABS * ROWS, SLOTS), 0) == row).astype(jnp.bfloat16)
    transposed = power.T
    high, low = bf16_parts(transposed)
    rest = (transposed - high.astype(jnp.float32) - low.astype(jnp.float32)).astype(jnp.bfloat16)
    table = dot(high, hot) + dot(low, hot) + dot(rest, hot)
    lane = lax.broadcasted_iota(jnp.int32, (LANES, SLOTS), 0)
    energy_ref[...] = jnp.sum(jnp.where(lane == pick, table, 0.0), axis=0, keepdims=True)


VMEM = pl.BlockSpec(memory_space=pltpu.VMEM)
SMEM = pl.BlockSpec(memory_space=pltpu.SMEM)


def band_index(y, x, core):
    return (y * 4 + x) * 2 + core


def gray(place):
    return place ^ (place >> 1)


PLACE_OF_CODE = [0, 1, 3, 2]


def neighbour(y, x, dim):
    code = gray(x) | (gray(y) << 2)
    code = code ^ (1 << dim)
    return PLACE_OF_CODE[code >> 2], PLACE_OF_CODE[code & 3]


def cube_pairs(slot, step):
    pairs = []
    for y in range(4):
        for x in range(4):
            for core in range(2):
                there = neighbour(y, x, (2 * core + slot + step) % 4)
                pairs.append((band_index(y, x, core), band_index(*there, core)))
    return pairs


CORE_PAIRS = [(i, i ^ 1) for i in range(32)]


def bit(code, position):
    return (code >> position) & 1


def broadcast_sources(orbitals, source_ids):
    me = lax.axis_index("band")
    core = me % 2
    x = (me // 2) % 4
    y = me // 8
    code = gray(x) | (gray(y) << 2)
    orbital = orbitals[0].reshape(2, 2, 2, 2, G, G)
    mine = lax.dynamic_index_in_dim(orbital, core, 0, keepdims=False)
    theirs = lax.ppermute(
        lax.dynamic_index_in_dim(orbital, 1 - core, 0, keepdims=False), "band", CORE_PAIRS
    )
    source_x = (source_ids // 2) % 4
    source_y = source_ids // 8
    relative = code ^ (gray(source_x) | (gray(source_y) << 2))
    is_mine = (source_ids % 2 == core)[:, None, None, None]

    def choose(slot, step):
        return jnp.where(flags[slot][step - 1], gots[slot], keeps[slot])

    places, partner_places, sides = [], [], []
    for slot in range(2):
        side = bit(code, (2 * core + slot) % 4)
        sides.append(side)
        partner_side = bit(code, (2 * (1 - core) + slot) % 4)
        places.append((4 * core + 2 * slot + side, 4 * core + 2 * slot + 1 - side))
        base = 4 * (1 - core) + 2 * slot
        partner_places.append((base + partner_side, base + 1 - partner_side))

    def half(slot, which):
        own = lax.dynamic_index_in_dim(mine[slot], which, 0, keepdims=False)
        other = lax.dynamic_index_in_dim(theirs[slot], which, 0, keepdims=False)
        return jnp.where(is_mine, own[None], other[None])

    def send(slot, value, step, name):
        return lax.ppermute(value, "band", CORE_PAIRS if name == "swap" else cube_pairs(slot, step))

    away = lax.optimization_barrier([half(slot, 1 - sides[slot]) for slot in range(2)])
    gots = [send(slot, away[slot], 0, "send") for slot in range(2)]
    keeps = lax.optimization_barrier([half(slot, sides[slot]) for slot in range(2)])
    flags = [
        [relative != 0] + [bit(relative, (2 * core + slot + step) % 4) == 1 for step in range(1, 4)]
        for slot in range(2)
    ]
    flags = jax.tree.map(lambda flag: flag[:, None, None, None], flags)
    flags = lax.optimization_barrier(flags)
    for step in range(1, 4):
        for slot in range(2):
            keeps[slot] = choose(slot, step)
            gots[slot] = send(slot, keeps[slot], step, "send")
    swapped, swapped_gots = [], []
    for slot in range(2):
        keeps[slot] = choose(slot, 4)
        gots[slot] = send(slot, keeps[slot], 4, "send")
        swapped.append(send(slot, keeps[slot], 4, "swap"))
    for slot in range(2):
        swapped_gots.append(send(slot, gots[slot], 5, "swap"))
    pieces = keeps + swapped + gots + swapped_gots
    order = [p[0] for p in places] + [p[0] for p in partner_places]
    order += [p[1] for p in places] + [p[1] for p in partner_places]
    return pieces, jnp.stack(order).astype(jnp.int32)


def call(kernel, specs, shapes):
    single = isinstance(shapes, jax.ShapeDtypeStruct)
    return pl.pallas_call(
        kernel,
        out_shape=shapes,
        in_specs=specs,
        out_specs=VMEM if single else tuple(VMEM for _ in shapes),
        compiler_params=pltpu.CompilerParams(vmem_limit_bytes=32 << 20),
    )


def turned(table, block, axis, join):
    forms = [np.roll(table, -block * slab, axis=axis) for slab in range(SLABS)]
    return jnp.asarray(np.stack([np.concatenate(split_table(form), axis=join) for form in forms]))


def turn(tables, slab):
    return lax.dynamic_index_in_dim(tables, slab, 0, keepdims=False)


FAR_ORDER = (4, 3, 5, 2, 6, 1, 7)


def exchange_blocks(blocks):
    came = [blocks[0]] + [None] * (SLABS - 1)
    for k in FAR_ORDER:
        pairs = [(z, (z + k) % SLABS) for z in range(SLABS)]
        came[SLABS - k] = lax.ppermute(blocks[k], "slab", pairs)
    return came


def step(orbitals, column_ids, source_ids):
    along_x, along_y, along_z = basis_tables()
    forward_y = turned(along_y, ROWS, 0, 0)
    forward_z = jnp.asarray(np.concatenate(split_table(along_z), axis=1))
    forward_x = turned(along_x, PLANES, 1, 0)
    inverse_x = turned(along_x.T, PLANES, 0, 1)
    inverse_y = turned(along_y.T, ROWS, 1, 1)
    inverse_z = jnp.asarray(np.stack(split_table(along_z.T), axis=0))

    f32 = jnp.float32
    slab = lax.axis_index("slab").astype(jnp.int32)
    slab_ref = slab.reshape(1)
    pieces, places = broadcast_sources(orbitals, source_ids)
    block = jax.ShapeDtypeStruct((PLANES, ROWS, LANES), f32)
    columns = call(
        forward_kernel, [SMEM] + [VMEM] * (3 + len(pieces)), (block,) * SLABS
    )(places, orbitals, turn(forward_y, slab), forward_z, *pieces)
    columns = exchange_blocks(columns)
    block = jax.ShapeDtypeStruct((PLANES + 1, ROWS, LANES), f32)
    back = call(
        filter_kernel, [SMEM] + [VMEM] * (2 + SLABS), (block,) * SLABS
    )(slab_ref, turn(forward_x, slab), turn(inverse_x, slab), *columns)
    back = exchange_blocks(back)
    exchange, energy = call(
        inverse_kernel,
        [SMEM] * 2 + [VMEM] * (3 + SLABS + len(pieces)),
        (
            jax.ShapeDtypeStruct((1, PLANES, G, G), f32),
            jax.ShapeDtypeStruct((1, SLOTS), f32),
        ),
    )(places, slab_ref, column_ids, turn(inverse_y, slab), inverse_z, *back, *pieces)
    return exchange, energy


def solution(mesh):
    placed = (P("band", "slab", None, None), P("slab", None), P())
    return jax.shard_map(
        step,
        mesh=mesh,
        in_specs=placed,
        out_specs=(P("band", "slab", None, None), P("band", "slab")),
        check_vma=False,
    )
```

```python
import math

import jax
import jax.numpy as jnp
import numpy as np
from jax import lax
from jax.experimental import pallas as pl
from jax.experimental.pallas import tpu as pltpu
from jax.sharding import PartitionSpec as P

G = 128
KCUT = 32
SLABS = 8
PLANES = 16
SLOTS = 768
ROWS = 8
LANES = 128


def split_table(table):
    high = table.astype(jnp.bfloat16)
    low = (table - high.astype(np.float64)).astype(jnp.bfloat16)
    return high, low


def waves(points):
    phase = np.arange(KCUT)[:, None] * np.arange(points)[None, :] % points
    angle = phase * (2.0 * math.pi / points)
    return np.cos(angle), np.sin(angle)


def basis_tables():
    cosine, sine = waves(G)
    along_x = np.concatenate([cosine, sine], axis=0)
    group_rows = []
    for slab in range(SLABS):
        group_rows.append(cosine[4 * slab : 4 * slab + 4])
        group_rows.append(sine[4 * slab : 4 * slab + 4])
    along_y = np.concatenate(group_rows, axis=0)
    along_z = np.zeros((2 * G, LANES))
    along_z[:G, :64] = along_x.T
    along_z[G:, 64:] = along_x.T
    return along_x, along_y, along_z


def bf16_parts(value):
    high = value.astype(jnp.bfloat16)
    low = (value - high.astype(jnp.float32)).astype(jnp.bfloat16)
    return high, low


def dot(a, b):
    return jnp.dot(a, b, preferred_element_type=jnp.float32)


def left_product(stacked, value):
    high, low = bf16_parts(value)
    rows = stacked.shape[0] // 2
    first = dot(stacked, high)
    return first[:rows] + first[rows:] + dot(stacked[:rows], low)


def wide_product(joined, value):
    high, low = bf16_parts(value)
    table = jnp.concatenate([joined, joined[:, :64]], axis=1)
    return dot(table, jnp.concatenate([high, high, low], axis=0))


def forward_kernel(place_ref, orbital_ref, ty_ref, tz_ref, *refs):
    piece_refs, out_refs = refs[:-SLABS], refs[-SLABS:]
    for p, piece_ref in enumerate(piece_refs):
        plane = place_ref[p] * 2
        orbital = orbital_ref[0, pl.ds(plane, 2)]
        pair0 = (piece_ref[0] * orbital).reshape(2 * G, G)
        pair1 = (piece_ref[1] * orbital).reshape(2 * G, G)
        high, low = bf16_parts(jnp.concatenate([pair0, pair1], axis=1))
        first = dot(high, tz_ref[...])
        along_z = first[:, :LANES] + first[:, LANES:] + dot(low, tz_ref[:, :LANES])
        for q in range(2):
            box = left_product(ty_ref[...], along_z[q * G : (q + 1) * G])
            for k in range(SLABS):
                out_refs[k][plane + q] = box[k * ROWS : (k + 1) * ROWS]


def filter_kernel(slab_ref, tx_ref, txt_ref, *refs):
    cols_refs, out_refs = refs[:SLABS], refs[SLABS:]

    def columns(j):
        return jnp.concatenate([ref[:, j, :] for ref in cols_refs], axis=0)

    lane = lax.broadcasted_iota(jnp.int32, (2 * KCUT, LANES), 1)
    row = lax.broadcasted_iota(jnp.int32, (2 * KCUT, LANES), 0)
    wave_z = lane % KCUT
    wave_x = row % KCUT
    scale = float(G) ** -3
    many_x = jnp.where(wave_x == 0, 1.0, 2.0)
    many_z = jnp.where(wave_z == 0, 1.0, 2.0)
    power_rows = []
    for j in range(4):
        wave_y = slab_ref[0] * 4 + j
        radius = wave_x * wave_x + wave_z * wave_z + wave_y * wave_y
        weight = jnp.where(
            radius < KCUT * KCUT, (4.0 * scale) / (1.0 + radius.astype(jnp.float32) / 1024.0), 0.0
        )
        weight = weight * many_x
        many_y = jnp.where(wave_y == 0, 1.0, 2.0)
        spread = weight * (many_z * many_y)
        cos_y = left_product(tx_ref[...], columns(j))
        sin_y = left_product(tx_ref[...], columns(j + 4))
        squares = jnp.sum(weight * (cos_y * cos_y + sin_y * sin_y), axis=0, keepdims=True)
        cross = cos_y * pltpu.roll(sin_y, 96, 1) - sin_y * pltpu.roll(cos_y, 96, 1)
        cross = 2.0 * jnp.sum(weight * cross, axis=0, keepdims=True)
        squares = squares + pltpu.roll(squares, 96, 1)
        same = squares - cross
        other = squares + cross
        same = same + pltpu.roll(same, 64, 1)
        other = other + pltpu.roll(other, 64, 1)
        first = lax.broadcasted_iota(jnp.int32, (1, LANES), 1) < KCUT
        power_rows.append(jnp.where(first, same, pltpu.roll(other, 32, 1)) * (1.0 / 64.0))
        for k, value in ((j, cos_y), (j + 4, sin_y)):
            back = wide_product(txt_ref[...], spread * value)
            for d in range(SLABS):
                out_refs[d][0:PLANES, k, :] = back[d * PLANES : (d + 1) * PLANES]
    power = jnp.concatenate(power_rows + power_rows, axis=0)
    for d in range(SLABS):
        out_refs[d][PLANES] = power


def inverse_kernel(place_ref, slab_ref, ids_ref, ty_ref, tz_ref, *refs):
    back_refs, piece_refs, exchange_ref, energy_ref = refs[:SLABS], refs[SLABS:-2], refs[-2], refs[-1]
    for p, piece_ref in enumerate(piece_refs):
        plane = place_ref[p] * 2
        rows = []
        for q in range(2):
            box = jnp.concatenate([ref[plane + q] for ref in back_refs], axis=0)
            rows.append(wide_product(ty_ref[...], box))
        high, low = bf16_parts(jnp.concatenate(rows, axis=0))
        pots = dot(jnp.concatenate([high, low], axis=1), tz_ref[: 2 * LANES]) + dot(high, tz_ref[2 * LANES :])
        value = piece_ref[0].reshape(2 * G, G) * pots[:, :G] + piece_ref[1].reshape(2 * G, G) * pots[:, G:]
        exchange_ref[0, pl.ds(plane, 2)] = value.reshape(2, G, G)
    power = jnp.concatenate([ref[PLANES] for ref in back_refs], axis=0)
    ids = ids_ref[...]
    wave_y = ids // 64 - KCUT
    wave_z = ids % 64 - KCUT
    size_y = jnp.abs(wave_y)
    size_z = jnp.abs(wave_z)
    group = (size_y // 4 + SLABS - slab_ref[0]) % SLABS
    row = jnp.where(size_y < KCUT, group * ROWS + size_y % 4, -1)
    pick = jnp.where(wave_y * wave_z < 0, size_z + KCUT, size_z)
    pick = jnp.where(size_z < KCUT, pick, -1)
    hot = (lax.broadcasted_iota(jnp.int32, (SLABS * ROWS, SLOTS), 0) == row).astype(jnp.bfloat16)
    transposed = power.T
    high, low = bf16_parts(transposed)
    rest = (transposed - high.astype(jnp.float32) - low.astype(jnp.float32)).astype(jnp.bfloat16)
    table = dot(high, hot) + dot(low, hot) + dot(rest, hot)
    lane = lax.broadcasted_iota(jnp.int32, (LANES, SLOTS), 0)
    energy_ref[...] = jnp.sum(jnp.where(lane == pick, table, 0.0), axis=0, keepdims=True)


VMEM = pl.BlockSpec(memory_space=pltpu.VMEM)
SMEM = pl.BlockSpec(memory_space=pltpu.SMEM)


def band_index(y, x, core):
    return (y * 4 + x) * 2 + core


def gray(place):
    return place ^ (place >> 1)


PLACE_OF_CODE = [0, 1, 3, 2]


def neighbour(y, x, dim):
    code = gray(x) | (gray(y) << 2)
    code = code ^ (1 << dim)
    return PLACE_OF_CODE[code >> 2], PLACE_OF_CODE[code & 3]


def cube_pairs(slot, step):
    pairs = []
    for y in range(4):
        for x in range(4):
            for core in range(2):
                there = neighbour(y, x, (2 * core + slot + step) % 4)
                pairs.append((band_index(y, x, core), band_index(*there, core)))
    return pairs


CORE_PAIRS = [(i, i ^ 1) for i in range(32)]


def bit(code, position):
    return (code >> position) & 1


def broadcast_sources(orbitals, source_ids):
    me = lax.axis_index("band")
    core = me % 2
    x = (me // 2) % 4
    y = me // 8
    code = gray(x) | (gray(y) << 2)
    source_x = (source_ids // 2) % 4
    source_y = source_ids // 8
    relative = code ^ (gray(source_x) | (gray(source_y) << 2))
    is_mine = (source_ids % 2 == core)[:, None, None, None]

    def choose(slot, step):
        return jnp.where(flags[slot][step - 1], gots[slot], keeps[slot])

    places, partner_places = [], []
    for slot in range(2):
        side = bit(code, (2 * core + slot) % 4)
        partner_side = bit(code, (2 * (1 - core) + slot) % 4)
        places.append((4 * core + 2 * slot + side, 4 * core + 2 * slot + 1 - side))
        base = 4 * (1 - core) + 2 * slot
        partner_places.append((base + partner_side, base + 1 - partner_side))

    def halves(orbitals, owner, away):
        parts = []
        for slot in range(2):
            side = bit(code, (2 * owner + slot) % 4)
            first = 8 * owner + 4 * slot + 2 * (1 - side if away else side)
            parts.append(lax.dynamic_slice_in_dim(orbitals[0], first, 2, 0))
        return parts

    def begin(orbitals, away):
        mine = halves(orbitals, core, away)
        theirs = lax.ppermute(jnp.stack(halves(orbitals, 1 - core, away)), "band", CORE_PAIRS)
        return [jnp.where(is_mine, mine[slot][None], theirs[slot][None]) for slot in range(2)]

    def send(slot, value, step, name):
        return lax.ppermute(value, "band", CORE_PAIRS if name == "swap" else cube_pairs(slot, step))

    away, later_orbitals = lax.optimization_barrier((begin(orbitals, True), orbitals))
    gots = [send(slot, away[slot], 0, "send") for slot in range(2)]
    keeps = list(lax.optimization_barrier(begin(later_orbitals, False)))
    flags = [
        [relative != 0] + [bit(relative, (2 * core + slot + step) % 4) == 1 for step in range(1, 4)]
        for slot in range(2)
    ]
    flags = jax.tree.map(lambda flag: flag[:, None, None, None], flags)
    flags = lax.optimization_barrier(flags)
    for step in range(1, 4):
        for slot in range(2):
            keeps[slot] = choose(slot, step)
            gots[slot] = send(slot, keeps[slot], step, "send")
    swapped, swapped_gots = [], []
    for slot in range(2):
        keeps[slot] = choose(slot, 4)
        gots[slot] = send(slot, keeps[slot], 4, "send")
        swapped.append(send(slot, keeps[slot], 4, "swap"))
    for slot in range(2):
        swapped_gots.append(send(slot, gots[slot], 5, "swap"))
    pieces = keeps + swapped + gots + swapped_gots
    order = [p[0] for p in places] + [p[0] for p in partner_places]
    order += [p[1] for p in places] + [p[1] for p in partner_places]
    return pieces, jnp.stack(order).astype(jnp.int32)


def call(kernel, specs, shapes):
    single = isinstance(shapes, jax.ShapeDtypeStruct)
    return pl.pallas_call(
        kernel,
        out_shape=shapes,
        in_specs=specs,
        out_specs=VMEM if single else tuple(VMEM for _ in shapes),
        compiler_params=pltpu.CompilerParams(vmem_limit_bytes=32 << 20),
    )


def turned(table, block, axis, join):
    forms = [np.roll(table, -block * slab, axis=axis) for slab in range(SLABS)]
    return jnp.asarray(np.stack([np.concatenate(split_table(form), axis=join) for form in forms]))


def turn(tables, slab):
    return lax.dynamic_index_in_dim(tables, slab, 0, keepdims=False)


FAR_ORDER = (4, 3, 5, 2, 6, 1, 7)


def exchange_blocks(blocks):
    came = [blocks[0]] + [None] * (SLABS - 1)
    for k in FAR_ORDER:
        pairs = [(z, (z + k) % SLABS) for z in range(SLABS)]
        came[SLABS - k] = lax.ppermute(blocks[k], "slab", pairs)
    return came


def step(orbitals, column_ids, source_ids):
    along_x, along_y, along_z = basis_tables()
    forward_y = turned(along_y, ROWS, 0, 0)
    forward_z = jnp.asarray(np.concatenate(split_table(along_z), axis=1))
    forward_x = turned(along_x, PLANES, 1, 0)
    inverse_x = turned(along_x.T, PLANES, 0, 1)
    inverse_y = turned(along_y.T, ROWS, 1, 1)
    high, low = split_table(along_z.T)
    inverse_z = jnp.asarray(np.concatenate([high, high, low], axis=0))

    f32 = jnp.float32
    slab = lax.axis_index("slab").astype(jnp.int32)
    slab_ref = slab.reshape(1)
    pieces, places = broadcast_sources(orbitals, source_ids)
    block = jax.ShapeDtypeStruct((PLANES, ROWS, LANES), f32)
    columns = call(
        forward_kernel, [SMEM] + [VMEM] * (3 + len(pieces)), (block,) * SLABS
    )(places, orbitals, turn(forward_y, slab), forward_z, *pieces)
    columns = exchange_blocks(columns)
    block = jax.ShapeDtypeStruct((PLANES + 1, ROWS, LANES), f32)
    back = call(
        filter_kernel, [SMEM] + [VMEM] * (2 + SLABS), (block,) * SLABS
    )(slab_ref, turn(forward_x, slab), turn(inverse_x, slab), *columns)
    back = exchange_blocks(back)
    exchange, energy = call(
        inverse_kernel,
        [SMEM] * 2 + [VMEM] * (3 + SLABS + len(pieces)),
        (
            jax.ShapeDtypeStruct((1, PLANES, G, G), f32),
            jax.ShapeDtypeStruct((1, SLOTS), f32),
        ),
    )(places, slab_ref, column_ids, turn(inverse_y, slab), inverse_z, *back, *pieces)
    return exchange, energy


def solution(mesh):
    placed = (P("band", "slab", None, None), P("slab", None), P())
    return jax.shard_map(
        step,
        mesh=mesh,
        in_specs=placed,
        out_specs=(P("band", "slab", None, None), P("band", "slab")),
        check_vma=False,
    )
```

```python
import math

import jax
import jax.numpy as jnp
import numpy as np
from jax import lax
from jax.experimental import pallas as pl
from jax.experimental.pallas import tpu as pltpu
from jax.sharding import PartitionSpec as P

G = 128
KCUT = 32
SLABS = 8
PLANES = 16
SLOTS = 768
ROWS = 8
LANES = 128
SENT = 7


def split_table(table):
    high = table.astype(jnp.bfloat16)
    low = (table - high.astype(np.float64)).astype(jnp.bfloat16)
    return high, low


def waves(points):
    phase = np.arange(KCUT)[:, None] * np.arange(points)[None, :] % points
    angle = phase * (2.0 * math.pi / points)
    return np.cos(angle), np.sin(angle)


def basis_tables():
    cosine, sine = waves(G)
    along_x = np.concatenate([cosine, sine], axis=0)
    group_rows = []
    for slab in range(SLABS):
        group_rows.append(cosine[4 * slab : 4 * slab + 4])
        group_rows.append(sine[4 * slab : 4 * slab + 4])
    along_y = np.concatenate(group_rows, axis=0)
    along_z = np.zeros((2 * G, LANES))
    along_z[:G, :64] = along_x.T
    along_z[G:, 64:] = along_x.T
    return along_x, along_y, along_z


def bf16_parts(value):
    high = value.astype(jnp.bfloat16)
    low = (value - high.astype(jnp.float32)).astype(jnp.bfloat16)
    return high, low


def dot(a, b):
    return jnp.dot(a, b, preferred_element_type=jnp.float32)


def left_product(stacked, value):
    high, low = bf16_parts(value)
    rows = stacked.shape[0] // 2
    first = dot(stacked, high)
    return first[:rows] + first[rows:] + dot(stacked[:rows], low)


def wide_product(joined, value):
    high, low = bf16_parts(value)
    table = jnp.concatenate([joined, joined[:, :64]], axis=1)
    return dot(table, jnp.concatenate([high, high, low], axis=0))


def sent_blocks(refs):
    home, pair, two, three, five, six, seven = refs
    return [home, pair.at[0], two, three, pair.at[1], five, six, seven]


def came_blocks(refs):
    home, one, two, three, far, six, near = refs
    return [home, one, two, three, far.at[1], far.at[0], six, near.at[0]]


def by_slab(steps, up):
    return [
        steps[k] if k % 4 == 0 else jnp.where(up, steps[k], steps[SLABS - k]) for k in range(SLABS)
    ]


def forward_kernel(place_ref, core_ref, orbital_ref, ty_ref, tz_ref, *refs):
    piece_refs, out_refs = refs[:-SENT], sent_blocks(refs[-SENT:])
    up = core_ref[0] == 1
    for p, piece_ref in enumerate(piece_refs):
        plane = place_ref[p] * 2
        orbital = orbital_ref[0, pl.ds(plane, 2)]
        pair0 = (piece_ref[0] * orbital).reshape(2 * G, G)
        pair1 = (piece_ref[1] * orbital).reshape(2 * G, G)
        high, low = bf16_parts(jnp.concatenate([pair0, pair1], axis=1))
        first = dot(high, tz_ref[...])
        along_z = first[:, :LANES] + first[:, LANES:] + dot(low, tz_ref[:, :LANES])
        for q in range(2):
            box = left_product(ty_ref[...], along_z[q * G : (q + 1) * G])
            blocks = by_slab([box[k * ROWS : (k + 1) * ROWS] for k in range(SLABS)], up)
            for k in range(SLABS):
                out_refs[k][plane + q] = blocks[k]


def filter_kernel(slab_ref, core_ref, tx_ref, txt_ref, *refs):
    cols_refs, out_refs = came_blocks(refs[:SENT]), sent_blocks(refs[SENT:])
    up = core_ref[0] == 1

    def columns(j):
        return jnp.concatenate(by_slab([ref[:, j, :] for ref in cols_refs], up), axis=0)

    lane = lax.broadcasted_iota(jnp.int32, (2 * KCUT, LANES), 1)
    row = lax.broadcasted_iota(jnp.int32, (2 * KCUT, LANES), 0)
    wave_z = lane % KCUT
    wave_x = row % KCUT
    scale = float(G) ** -3
    many_x = jnp.where(wave_x == 0, 1.0, 2.0)
    many_z = jnp.where(wave_z == 0, 1.0, 2.0)
    power_rows = []
    for j in range(4):
        wave_y = slab_ref[0] * 4 + j
        radius = wave_x * wave_x + wave_z * wave_z + wave_y * wave_y
        weight = jnp.where(
            radius < KCUT * KCUT, (4.0 * scale) / (1.0 + radius.astype(jnp.float32) / 1024.0), 0.0
        )
        weight = weight * many_x
        many_y = jnp.where(wave_y == 0, 1.0, 2.0)
        spread = weight * (many_z * many_y)
        cos_y = left_product(tx_ref[...], columns(j))
        sin_y = left_product(tx_ref[...], columns(j + 4))
        squares = jnp.sum(weight * (cos_y * cos_y + sin_y * sin_y), axis=0, keepdims=True)
        cross = cos_y * pltpu.roll(sin_y, 96, 1) - sin_y * pltpu.roll(cos_y, 96, 1)
        cross = 2.0 * jnp.sum(weight * cross, axis=0, keepdims=True)
        squares = squares + pltpu.roll(squares, 96, 1)
        same = squares - cross
        other = squares + cross
        same = same + pltpu.roll(same, 64, 1)
        other = other + pltpu.roll(other, 64, 1)
        first = lax.broadcasted_iota(jnp.int32, (1, LANES), 1) < KCUT
        power_rows.append(jnp.where(first, same, pltpu.roll(other, 32, 1)) * (1.0 / 64.0))
        for k, value in ((j, cos_y), (j + 4, sin_y)):
            back = wide_product(txt_ref[...], spread * value)
            blocks = by_slab([back[d * PLANES : (d + 1) * PLANES] for d in range(SLABS)], up)
            for d in range(SLABS):
                out_refs[d][0:PLANES, k, :] = blocks[d]
    power = jnp.concatenate(power_rows + power_rows, axis=0)
    for d in range(SLABS):
        out_refs[d][PLANES] = power


def inverse_kernel(place_ref, slab_ref, core_ref, ids_ref, ty_ref, tz_ref, *refs):
    back_refs, piece_refs, exchange_ref, energy_ref = refs[:SENT], refs[SENT:-2], refs[-2], refs[-1]
    back_refs = came_blocks(back_refs)
    up = core_ref[0] == 1
    for p, piece_ref in enumerate(piece_refs):
        plane = place_ref[p] * 2
        rows = []
        for q in range(2):
            box = jnp.concatenate(by_slab([ref[plane + q] for ref in back_refs], up), axis=0)
            rows.append(wide_product(ty_ref[...], box))
        high, low = bf16_parts(jnp.concatenate(rows, axis=0))
        pots = dot(jnp.concatenate([high, low], axis=1), tz_ref[: 2 * LANES]) + dot(high, tz_ref[2 * LANES :])
        value = piece_ref[0].reshape(2 * G, G) * pots[:, :G] + piece_ref[1].reshape(2 * G, G) * pots[:, G:]
        exchange_ref[0, pl.ds(plane, 2)] = value.reshape(2, G, G)
    power = jnp.concatenate(by_slab([ref[PLANES] for ref in back_refs], up), axis=0)
    ids = ids_ref[...]
    wave_y = ids // 64 - KCUT
    wave_z = ids % 64 - KCUT
    size_y = jnp.abs(wave_y)
    size_z = jnp.abs(wave_z)
    group = (size_y // 4 + SLABS - slab_ref[0]) % SLABS
    row = jnp.where(size_y < KCUT, group * ROWS + size_y % 4, -1)
    pick = jnp.where(wave_y * wave_z < 0, size_z + KCUT, size_z)
    pick = jnp.where(size_z < KCUT, pick, -1)
    hot = (lax.broadcasted_iota(jnp.int32, (SLABS * ROWS, SLOTS), 0) == row).astype(jnp.bfloat16)
    transposed = power.T
    high, low = bf16_parts(transposed)
    rest = (transposed - high.astype(jnp.float32) - low.astype(jnp.float32)).astype(jnp.bfloat16)
    table = dot(high, hot) + dot(low, hot) + dot(rest, hot)
    lane = lax.broadcasted_iota(jnp.int32, (LANES, SLOTS), 0)
    energy_ref[...] = jnp.sum(jnp.where(lane == pick, table, 0.0), axis=0, keepdims=True)


VMEM = pl.BlockSpec(memory_space=pltpu.VMEM)
SMEM = pl.BlockSpec(memory_space=pltpu.SMEM)


def band_index(y, x, core):
    return (y * 4 + x) * 2 + core


def gray(place):
    return place ^ (place >> 1)


PLACE_OF_CODE = [0, 1, 3, 2]


def neighbour(y, x, dim):
    code = gray(x) | (gray(y) << 2)
    code = code ^ (1 << dim)
    return PLACE_OF_CODE[code >> 2], PLACE_OF_CODE[code & 3]


def cube_pairs(slot, step):
    pairs = []
    for y in range(4):
        for x in range(4):
            for core in range(2):
                there = neighbour(y, x, (2 * core + slot + step) % 4)
                pairs.append((band_index(y, x, core), band_index(*there, core)))
    return pairs


CORE_PAIRS = [(i, i ^ 1) for i in range(32)]


def bit(code, position):
    return (code >> position) & 1


def broadcast_sources(orbitals, source_ids):
    me = lax.axis_index("band")
    core = me % 2
    x = (me // 2) % 4
    y = me // 8
    code = gray(x) | (gray(y) << 2)
    source_x = (source_ids // 2) % 4
    source_y = source_ids // 8
    relative = code ^ (gray(source_x) | (gray(source_y) << 2))
    is_mine = (source_ids % 2 == core)[:, None, None, None]

    def choose(slot, step):
        return jnp.where(flags[slot][step - 1], gots[slot], keeps[slot])

    places, partner_places = [], []
    for slot in range(2):
        side = bit(code, (2 * core + slot) % 4)
        partner_side = bit(code, (2 * (1 - core) + slot) % 4)
        places.append((4 * core + 2 * slot + side, 4 * core + 2 * slot + 1 - side))
        base = 4 * (1 - core) + 2 * slot
        partner_places.append((base + partner_side, base + 1 - partner_side))

    def halves(orbitals, owner, away):
        parts = []
        for slot in range(2):
            side = bit(code, (2 * owner + slot) % 4)
            first = 8 * owner + 4 * slot + 2 * (1 - side if away else side)
            parts.append(lax.dynamic_slice_in_dim(orbitals[0], first, 2, 0))
        return parts

    def begin(orbitals, away):
        mine = halves(orbitals, core, away)
        theirs = lax.ppermute(jnp.stack(halves(orbitals, 1 - core, away)), "band", CORE_PAIRS)
        return [jnp.where(is_mine, mine[slot][None], theirs[slot][None]) for slot in range(2)]

    def send(slot, value, step, name):
        return lax.ppermute(value, "band", CORE_PAIRS if name == "swap" else cube_pairs(slot, step))

    away, later_orbitals = lax.optimization_barrier((begin(orbitals, True), orbitals))
    gots = [send(slot, away[slot], 0, "send") for slot in range(2)]
    keeps = list(lax.optimization_barrier(begin(later_orbitals, False)))
    flags = [
        [relative != 0] + [bit(relative, (2 * core + slot + step) % 4) == 1 for step in range(1, 4)]
        for slot in range(2)
    ]
    flags = jax.tree.map(lambda flag: flag[:, None, None, None], flags)
    flags = lax.optimization_barrier(flags)
    for step in range(1, 4):
        for slot in range(2):
            keeps[slot] = choose(slot, step)
            gots[slot] = send(slot, keeps[slot], step, "send")
    swapped, swapped_gots = [], []
    for slot in range(2):
        keeps[slot] = choose(slot, 4)
        gots[slot] = send(slot, keeps[slot], 4, "send")
        swapped.append(send(slot, keeps[slot], 4, "swap"))
    for slot in range(2):
        swapped_gots.append(send(slot, gots[slot], 5, "swap"))
    pieces = keeps + swapped + gots + swapped_gots
    order = [p[0] for p in places] + [p[0] for p in partner_places]
    order += [p[1] for p in places] + [p[1] for p in partner_places]
    return pieces, jnp.stack(order).astype(jnp.int32)


def call(kernel, specs, shapes):
    single = isinstance(shapes, jax.ShapeDtypeStruct)
    return pl.pallas_call(
        kernel,
        out_shape=shapes,
        in_specs=specs,
        out_specs=VMEM if single else tuple(VMEM for _ in shapes),
        compiler_params=pltpu.CompilerParams(vmem_limit_bytes=32 << 20),
    )


def turned(table, block, axis, join):
    forms = [np.roll(table, -block * slab, axis=axis) for slab in range(SLABS)]
    return jnp.asarray(np.stack([np.concatenate(split_table(form), axis=join) for form in forms]))


def turn(tables, slab):
    return lax.dynamic_index_in_dim(tables, slab, 0, keepdims=False)


def exchange_blocks(blocks):
    home, pair, two, three, five, six, seven = blocks

    def send(value, steps):
        pairs = []
        for band in range(32):
            ahead = steps if band % 2 else -steps
            for z in range(SLABS):
                pairs.append((band * SLABS + z, band * SLABS + (z + ahead) % SLABS))
        return lax.ppermute(value, ("band", "slab"), pairs)

    near = send(pair, 1)
    three_back = send(five, -3)
    far = send(jnp.stack([three, near[1]]), 3)
    six_here = send(two, 2)
    two_here = send(six, -2)
    one_here = send(seven, -1)
    return [home, one_here, two_here, three_back, far, six_here, near]


def sent_shapes(block):
    pair = jax.ShapeDtypeStruct((2,) + block.shape, block.dtype)
    return (block, pair) + (block,) * 5


def step(orbitals, column_ids, source_ids):
    along_x, along_y, along_z = basis_tables()
    forward_y = turned(along_y, ROWS, 0, 0)
    forward_z = jnp.asarray(np.concatenate(split_table(along_z), axis=1))
    forward_x = turned(along_x, PLANES, 1, 0)
    inverse_x = turned(along_x.T, PLANES, 0, 1)
    inverse_y = turned(along_y.T, ROWS, 1, 1)
    high, low = split_table(along_z.T)
    inverse_z = jnp.asarray(np.concatenate([high, high, low], axis=0))

    f32 = jnp.float32
    slab = lax.axis_index("slab").astype(jnp.int32)
    slab_ref = slab.reshape(1)
    pieces, places = broadcast_sources(orbitals, source_ids)
    block = jax.ShapeDtypeStruct((PLANES, ROWS, LANES), f32)
    core = (lax.axis_index("band") % 2).astype(jnp.int32).reshape(1)
    columns = call(
        forward_kernel, [SMEM] * 2 + [VMEM] * (3 + len(pieces)), sent_shapes(block)
    )(places, core, orbitals, turn(forward_y, slab), forward_z, *pieces)
    columns = exchange_blocks(columns)
    block = jax.ShapeDtypeStruct((PLANES + 1, ROWS, LANES), f32)
    back = call(
        filter_kernel, [SMEM] * 2 + [VMEM] * (2 + SENT), sent_shapes(block)
    )(slab_ref, core, turn(forward_x, slab), turn(inverse_x, slab), *columns)
    back = exchange_blocks(back)
    exchange, energy = call(
        inverse_kernel,
        [SMEM] * 3 + [VMEM] * (3 + SENT + len(pieces)),
        (
            jax.ShapeDtypeStruct((1, PLANES, G, G), f32),
            jax.ShapeDtypeStruct((1, SLOTS), f32),
        ),
    )(places, slab_ref, core, column_ids, turn(inverse_y, slab), inverse_z, *back, *pieces)
    return exchange, energy


def solution(mesh):
    placed = (P("band", "slab", None, None), P("slab", None), P())
    return jax.shard_map(
        step,
        mesh=mesh,
        in_specs=placed,
        out_specs=(P("band", "slab", None, None), P("band", "slab")),
        check_vma=False,
    )
```
